256 devices in a mesh: tm: 16 (over y, x), rows: 8 (over z), cols: 2 (over core).
Axes of the slice: x: 4, y: 4, z: 8, core: 2. Of those that a mesh axis runs over, the one named last changes fastest.
Arguments:
- latent_video: bfloat16 [96, 256, 64, 128], P('tm', 'rows', 'cols'), may hold values from -6 to 6
- input_kernel: bfloat16 [3, 3, 128, 256], replicated, may hold values from -0.1875 to 0.1875
- output_kernel: bfloat16 [3, 3, 256, 128], replicated, may hold values from -0.125 to 0.125
- decay_rate: float32 [96, 256], P('tm'), may hold values from 0.4 to 0.999, as said below
- skip_gain: float32 [128], replicated, may hold values from 0.25 to 1.75
Outputs:
- layer_output: bfloat16 [96, 256, 64, 128], P('tm', 'rows', 'cols')
The draws below stay inside these ranges and needn't reach their ends.
Inputs may be any that keep to these rules, and one draw needn't show every extreme that they name: `decay_rate`: every decay factor lies strictly between zero and one.
All inputs are finite; a program needn't handle non-finite values.
Results may differ from the reference program's by a relative error of at most 0.0048.
Values may be sent and summed in bfloat16 or wider, within the bound.
No kernel may reach another device: no remote copies, remote signals or barrier semaphores. Data moves between devices by JAX's collectives and lax.ppermute only.
A program may use at most 128 MiB of HBM per device.

```python
import jax
import jax.numpy as jnp
from jax import lax

CIN = 128
STATE = 256
TOTAL_FRAMES = 96
HEIGHT = 256
WIDTH = 64


def draw_decay_rate(key, part):
    random_seeds = jax.random.split(jax.random.fold_in(key, 17), 6)
    fast = jax.random.bernoulli(random_seeds[0], 0.5, (STATE,))
    slow_loss = jax.random.uniform(random_seeds[1], (STATE,), jnp.float32, 0.02, 0.4)
    slow_rate = jnp.exp(-slow_loss / TOTAL_FRAMES)
    fast_span = jax.random.uniform(random_seeds[2], (STATE,), jnp.float32, 30.0, 50.0)
    fast_rate = jnp.exp(-2.302585 / fast_span)
    baseline_forget = jnp.where(fast, fast_rate, slow_rate)
    jitter_loss = jax.random.uniform(random_seeds[3], (TOTAL_FRAMES, STATE), jnp.float32, 0.0, 0.3)
    wobble_factor = jnp.exp(-jitter_loss / TOTAL_FRAMES)
    spike_frames = jax.random.randint(random_seeds[4], (2,), 0, TOTAL_FRAMES)
    frame_numbers = jnp.arange(TOTAL_FRAMES, dtype=jnp.int32)
    spike_flag = jnp.any(frame_numbers[:, None] == spike_frames[None, :], axis=1)[:, None]
    spike_scale = jax.random.uniform(random_seeds[5], (TOTAL_FRAMES, 1), jnp.float32, 0.55, 0.8)
    forget_speeds = baseline_forget[None, :] * wobble_factor * jnp.where(spike_flag, spike_scale, 1.0)
    return jnp.clip(forget_speeds, 0.25, 0.999).astype(jnp.float32)


def level_of(own_key, extent, pieces, smallest, top_value):
    factor_of, own = 1.0, jax.random.fold_in(own_key, 6)
    for axis_at, shards_of in pieces:
        steps = jnp.exp(jax.random.uniform(jax.random.fold_in(own, axis_at), (shards_of,), jnp.float32, smallest / len(pieces), top_value / len(pieces)))
        factor_of = factor_of * jnp.repeat(steps, extent[axis_at] // shards_of).reshape([-1 if axis == axis_at else 1 for axis in range(len(extent))])
    return factor_of


def centred(key, shape, deviation, bound, cuts=(), kind=jnp.bfloat16):
    gain = level_of(key, shape, cuts, -0.22, 0.18) if cuts else 1.0
    drawn = jax.random.normal(key, shape, jnp.float32) * deviation * gain
    return jnp.minimum(jnp.maximum(drawn, -bound), bound).astype(kind)


def setup_inputs(seed: int = 0) -> dict:
    key_list = jax.random.split(jax.random.key(seed), 6)
    return {
        "latent_video": centred(key_list[0], (TOTAL_FRAMES, HEIGHT, WIDTH, CIN), 1.0, 6.0, ((0, 16), (1, 8), (2, 2))),
        "input_kernel": centred(key_list[1], (3, 3, CIN, STATE), (9 * CIN) ** -0.5, 0.1875),
        "output_kernel": centred(key_list[2], (3, 3, STATE, CIN), (9 * STATE) ** -0.5, 0.125),
        "decay_rate": draw_decay_rate(jax.random.fold_in(key_list[5], 71), 0),
        "skip_gain": jnp.clip(1.0 + 0.15 * jax.random.normal(key_list[4], (CIN,), jnp.float32), 0.25, 1.75),
    }


def stencil(field, kernel):
    height = field.shape[1] - 2
    width = field.shape[2] - 2
    summed = jnp.zeros((field.shape[0], height, width, kernel.shape[3]), jnp.float32)
    for row_off in range(3):
        for col_off in range(3):
            window = field[:, row_off:row_off + height, col_off:col_off + width, :].astype(jnp.float32)
            summed = summed + jnp.einsum("fhwc,cs->fhws", window, kernel[row_off, col_off].astype(jnp.float32))
    return summed


def advance(running, inputs):
    drive_now, rate_now = inputs
    running = rate_now * running + drive_now
    return running, running


def reference(latent_video, input_kernel, output_kernel, decay_rate, skip_gain):
    padded = jnp.pad(latent_video, ((0, 0), (1, 1), (1, 1), (0, 0)))
    drive = stencil(padded, input_kernel)
    start = jnp.zeros((HEIGHT, WIDTH, STATE), jnp.float32)
    last_state, states = lax.scan(advance, start, (drive, decay_rate))
    rounded_states = states.astype(jnp.bfloat16)
    cycle = jnp.pad(rounded_states, ((0, 0), (1, 1), (1, 1), (0, 0)))
    mixed = stencil(cycle, output_kernel) + skip_gain * latent_video.astype(jnp.float32)
    return mixed.astype(jnp.bfloat16)
```

```python
import jax
import jax.numpy as jnp
from jax import lax
from jax.experimental import pallas as pl
from jax.experimental.pallas import tpu as pltpu
from jax.sharding import Mesh
from jax.sharding import PartitionSpec as P

TM = ("tm_0", "tm_1")
SIDE = 4
FRAMES, ROWS, COLS, CIN, STATE = 6, 32, 32, 128, 256
WIDE = ROWS + 2
TALL = ROWS + 4
MAIN = WIDE * COLS
EDGE = 48
EDGE_IN = 64
ALL = MAIN + EDGE
PIECE = 288
PADDED = SIDE * PIECE
SENT = PIECE + 16

f32, bf16 = jnp.float32, jnp.bfloat16


def split3(value):
    high = value.astype(bf16)
    rest = value - high.astype(f32)
    mid = rest.astype(bf16)
    low = (rest - mid.astype(f32)).astype(bf16)
    row = lax.broadcasted_iota(jnp.int32, (16, STATE), 0)
    tile = jnp.where(row == 0, high.astype(f32), 0.0)
    tile = jnp.where(row == 1, mid.astype(f32), tile)
    tile = jnp.where(row == 2, low.astype(f32), tile)
    return tile.astype(bf16)


def joined(tile):
    tile = tile.astype(f32)
    return tile[0:1] + tile[1:2] + tile[2:3]


def turned(here, k):
    return lax.rem(here + k + SIDE, SIDE)


def shifted(row, amount, where_at, edge):
    moved = pltpu.roll(row, amount, 0)
    at = lax.broadcasted_iota(jnp.int32, row.shape, 0)
    return jnp.where(at == where_at, edge, moved).astype(bf16)


def drive_kernel(x_ref, top_ref, low_ref, own_ref, near_ref, kernel_ref, decay_ref, drive_ref,
                 c0_ref, c1_ref, c2_ref, c3_ref, wide_ref, running_ref, last_ref):
    t = pl.program_id(0)
    on_left = lax.axis_index("cols") == 0
    is_left = on_left.astype(f32)
    is_right = 1.0 - is_left
    row_tile = lax.axis_index("rows")
    top_ok = (row_tile > 0).astype(f32)
    low_ok = (row_tile < lax.axis_size("rows") - 1).astype(f32)
    own0 = own_ref[0, 0].astype(f32)
    own1 = own_ref[0, 1].astype(f32)
    near0 = near_ref[0, 0].astype(f32)
    near1 = near_ref[0, 1].astype(f32)
    left_halo = near1 * is_right
    right_halo = near0 * is_left
    for h in range(TALL):
        if h < 2:
            row = top_ref[0, h]
        elif h < ROWS + 2:
            row = x_ref[0, h - 2]
        else:
            row = low_ref[0, h - ROWS - 2]
        at = pl.ds(h * COLS, COLS)
        wide = row.astype(f32)
        wide_ref[at, 0:CIN] = shifted(wide, 1, 0, left_halo[h:h + 1])
        wide_ref[at, CIN:2 * CIN] = row
        wide_ref[at, 2 * CIN:3 * CIN] = shifted(wide, COLS - 1, COLS - 1, right_halo[h:h + 1])
    sides = [
        own1 * is_left + near0 * is_right,
        near0 * is_left + near1 * is_right,
        near1 * is_left + own0 * is_right,
    ]
    edge = jnp.concatenate(
        [side[a:a + EDGE].astype(bf16) for a in range(3) for side in sides], axis=1
    )
    main = jnp.concatenate([wide_ref[a * COLS:a * COLS + MAIN, :] for a in range(3)], axis=1)
    drive_ref[0, 0:MAIN] = jnp.dot(main, kernel_ref[...], preferred_element_type=f32)
    drive_ref[0, MAIN:ALL] = jnp.dot(edge, kernel_ref[...], preferred_element_type=f32)
    drive_ref[0, 0:COLS] = drive_ref[0, 0:COLS] * top_ok
    drive_ref[0, MAIN - COLS:MAIN] = drive_ref[0, MAIN - COLS:MAIN] * low_ok
    at = lax.broadcasted_iota(jnp.int32, (EDGE, STATE), 0)
    keep = jnp.where(at == 0, top_ok, jnp.where(at == WIDE - 1, low_ok, 1.0))
    drive_ref[0, MAIN:ALL] = drive_ref[0, MAIN:ALL] * keep

    @pl.when(t == 0)
    def _():
        running_ref[...] = drive_ref[0]

    @pl.when(t > 0)
    def _():
        running_ref[...] = running_ref[...] * decay_ref[pl.ds(t, 1), :] + drive_ref[0]

    @pl.when(t == FRAMES - 1)
    def _():
        last_ref[0:ALL] = running_ref[...].astype(bf16)
        last_ref[ALL:PADDED] = jnp.zeros((PADDED - ALL, STATE), bf16)
        product = decay_ref[0:1, :]
        for k in range(1, FRAMES):
            product = product * decay_ref[k:k + 1, :]
        tile = split3(product)
        here = lax.axis_index("tm_1")
        for k, out in enumerate((c0_ref, c1_ref, c2_ref, c3_ref)):
            first = pl.multiple_of(turned(here, k) * PIECE, 16)
            out[0:PIECE] = last_ref[pl.ds(first, PIECE), :]
            out[PIECE:SENT] = tile


def total_kernel(r0, r1, r2, r3, total_ref, held):
    here = lax.axis_index("tm_1")
    for k, got in enumerate((r0, r1, r2, r3)):
        held[turned(here, -k)] = got[...]
    total = held[0, 0:PIECE].astype(f32)
    product = joined(held[0, PIECE:SENT])
    for j in range(1, SIDE):
        rate = joined(held[j, PIECE:SENT])
        total = total * rate + held[j, 0:PIECE].astype(f32)
        product = product * rate
    total_ref[0:PIECE] = total.astype(bf16)
    total_ref[PIECE:SENT] = split3(product)


def enter_kernel(r0, r1, r2, r3, s1, s2, s3, e0, e1, e2, e3, held, above, before, entering):
    x = lax.axis_index("tm_1")
    y = lax.axis_index("tm_0")
    for k, got in enumerate((r0, r1, r2, r3)):
        held[turned(x, -k)] = got[...]
    for k, got in enumerate((s1, s2, s3)):
        above[turned(y, -(k + 1))] = got[...]
    before[...] = jnp.zeros((PIECE, STATE), f32)

    def one(j, _):
        before[...] = before[...] * joined(above[j, PIECE:SENT]) + above[j, 0:PIECE].astype(f32)
        return 0

    lax.fori_loop(0, y, one, 0)
    value = before[...]
    for j in range(SIDE):
        entering[j] = value.astype(bf16)
        if j < SIDE - 1:
            value = value * joined(held[j, PIECE:SENT]) + held[j, 0:PIECE].astype(f32)
    for k, out in enumerate((e0, e1, e2, e3)):
        out[...] = entering[turned(x, k)]


def output_kernel_body(f0, f1, f2, f3, drive_ref, decay_ref, kernel_ref, gain_ref, x_ref, out_ref,
                       start_ref, running_ref, state_ref):
    t = pl.program_id(0)
    on_left = lax.axis_index("cols") == 0
    is_left = on_left.astype(f32)
    is_right = 1.0 - is_left

    @pl.when(t == 0)
    def _():
        here = lax.axis_index("tm_1")
        for k, got in enumerate((f0, f1, f2, f3)):
            first = pl.multiple_of(turned(here, -k) * PIECE, 16)
            start_ref[pl.ds(first, PIECE), :] = got[...]
        running_ref[...] = start_ref[0:ALL].astype(f32)

    rate = decay_ref[pl.ds(t, 1), :]
    edge = running_ref[MAIN:ALL] * rate + drive_ref[0, MAIN:ALL]
    running_ref[MAIN:ALL] = edge
    left_edge = edge * is_right
    right_edge = edge * is_left
    for h in range(WIDE):
        at = pl.ds(h * COLS, COLS)
        row = running_ref[at, :] * rate + drive_ref[0, at, :]
        running_ref[at, :] = row
        state_ref[0, h] = shifted(row, 1, 0, left_edge[h:h + 1])
        state_ref[1, h] = row.astype(bf16)
        state_ref[2, h] = shifted(row, COLS - 1, COLS - 1, right_edge[h:h + 1])
    parts = []
    for r in range(4):
        for b in range(3):
            rows = [state_ref[b, 2 * hp + r] for hp in range(ROWS // 2)]
            parts.append(jnp.concatenate(rows, axis=0))
    cycle = jnp.concatenate(parts, axis=1)
    mixed = jnp.dot(cycle, kernel_ref[...], preferred_element_type=f32)
    gain = gain_ref[...]
    for h in range(ROWS):
        part = mixed[(h // 2) * COLS:(h // 2 + 1) * COLS, (h % 2) * CIN:(h % 2 + 1) * CIN]
        out_ref[0, h] = (part + gain * x_ref[0, h].astype(f32)).astype(bf16)


def params():
    return pltpu.CompilerParams(vmem_limit_bytes=48 * 1024 * 1024)


def whole():
    return pl.BlockSpec(memory_space=pltpu.VMEM)


def framed(*shape):
    return pl.BlockSpec((1,) + shape, lambda t: (t,) + (0,) * len(shape))


def fixed(*shape):
    return pl.BlockSpec(shape, lambda t: (0,) * len(shape))


def spread(value, axis):
    return [
        lax.ppermute(value[k] if isinstance(value, (list, tuple)) else value, axis,
                     [(i, (i + k + 1) % SIDE) for i in range(SIDE)])
        for k in range(SIDE - 1)
    ]


def on_device(latent_video, input_kernel, output_kernel, decay_rate, skip_gain):
    x = latent_video
    count = lax.axis_size("rows")
    forward = [(i, i + 1) for i in range(count - 1)]
    backward = [(i + 1, i) for i in range(count - 1)]
    top = lax.ppermute(x[:, ROWS - 2:], "rows", forward)
    low = lax.ppermute(x[:, :2], "rows", backward)
    on_left = lax.axis_index("cols") == 0

    def edge_of(part):
        return jnp.where(on_left, part[:, :, COLS - 2:], part[:, :, :2])

    own = jnp.concatenate([edge_of(top), edge_of(x), edge_of(low)], axis=1)
    own = jnp.pad(own.transpose(0, 2, 1, 3), ((0, 0), (0, 0), (0, EDGE_IN - TALL), (0, 0)))
    near = lax.ppermute(own, "cols", [(0, 1), (1, 0)])

    piece = jax.ShapeDtypeStruct((SENT, STATE), bf16)
    drive, c0, c1, c2, c3 = pl.pallas_call(
        drive_kernel,
        grid=(FRAMES,),
        out_shape=[jax.ShapeDtypeStruct((FRAMES, ALL, STATE), f32)] + [piece] * SIDE,
        in_specs=[
            framed(ROWS, COLS, CIN), framed(2, COLS, CIN), framed(2, COLS, CIN),
            framed(2, EDGE_IN, CIN), framed(2, EDGE_IN, CIN),
            fixed(9 * CIN, STATE), fixed(FRAMES, STATE),
        ],
        out_specs=[framed(ALL, STATE)] + [fixed(SENT, STATE)] * SIDE,
        scratch_shapes=[
            pltpu.VMEM((TALL * COLS, 3 * CIN), bf16),
            pltpu.VMEM((ALL, STATE), f32),
            pltpu.VMEM((PADDED, STATE), bf16),
        ],
        compiler_params=params(),
        name="drive",
    )(x, top, low, own, near, input_kernel.reshape(9 * CIN, STATE), decay_rate)

    r1, r2, r3 = spread((c1, c2, c3), "tm_1")
    total = pl.pallas_call(
        total_kernel,
        out_shape=piece,
        in_specs=[whole()] * 4,
        out_specs=whole(),
        scratch_shapes=[pltpu.VMEM((SIDE, SENT, STATE), bf16)],
        compiler_params=params(),
        name="total",
    )(c0, r1, r2, r3)
    s1, s2, s3 = spread(total, "tm_0")
    e0, e1, e2, e3 = pl.pallas_call(
        enter_kernel,
        out_shape=[jax.ShapeDtypeStruct((PIECE, STATE), bf16)] * SIDE,
        in_specs=[whole()] * 7,
        out_specs=[whole()] * SIDE,
        scratch_shapes=[
            pltpu.VMEM((SIDE, SENT, STATE), bf16),
            pltpu.VMEM((SIDE, SENT, STATE), bf16),
            pltpu.VMEM((PIECE, STATE), f32),
            pltpu.VMEM((SIDE, PIECE, STATE), bf16),
        ],
        compiler_params=params(),
        name="enter",
    )(c0, r1, r2, r3, s1, s2, s3)
    f1, f2, f3 = spread((e1, e2, e3), "tm_1")

    taps = output_kernel.reshape(3, 3 * STATE, CIN)
    blank = jnp.zeros((1, 3 * STATE, CIN), bf16)
    pair = jnp.concatenate(
        [jnp.concatenate([taps, blank], axis=0), jnp.concatenate([blank, taps], axis=0)], axis=2
    ).reshape(12 * STATE, 2 * CIN)

    return pl.pallas_call(
        output_kernel_body,
        grid=(FRAMES,),
        out_shape=jax.ShapeDtypeStruct((FRAMES, ROWS, COLS, CIN), bf16),
        in_specs=[fixed(PIECE, STATE)] * 4 + [
            framed(ALL, STATE), fixed(FRAMES, STATE), fixed(12 * STATE, 2 * CIN), fixed(1, CIN),
            framed(ROWS, COLS, CIN),
        ],
        out_specs=framed(ROWS, COLS, CIN),
        scratch_shapes=[
            pltpu.VMEM((PADDED, STATE), bf16),
            pltpu.VMEM((ALL, STATE), f32),
            pltpu.VMEM((3, WIDE, COLS, STATE), bf16),
        ],
        compiler_params=params(),
        name="output",
    )(e0, f1, f2, f3, drive, decay_rate, pair, skip_gain.reshape(1, CIN), x)


def solution(mesh):
    finer = Mesh(
        mesh.devices.reshape(4, 4, mesh.shape["rows"], mesh.shape["cols"]),
        ("tm_0", "tm_1", "rows", "cols"),
    )
    placed = (P(TM, "rows", "cols", None), P(), P(), P(TM, None), P())
    return jax.shard_map(
        on_device,
        mesh=finer,
        in_specs=placed,
        out_specs=P(TM, "rows", "cols", None),
        check_vma=False,
    )
```
